256 devices in a mesh: mirror: 2 (over y_hi), slab: 64 (over z, y_lo, x), cols: 2 (over core).
Axes of the slice: x: 4, y: 4 (y_hi: 2, y_lo: 2; y = y_hi * 2 + y_lo), z: 8, core: 2. Of those that a mesh axis runs over, the one named last changes fastest.
Arguments:
- right_side: float32 [2, 1024, 65536], P('mirror', 'slab', 'cols'), parts along dimension 2, may hold values from -6 to 6
- analysis: float32 [2, 1024, 1024], P('mirror'), may hold values from -0.1875 to 0.1875
- synthesis: float32 [2, 1024, 1024], P('mirror'), may hold values from -0.1875 to 0.1875
- negated_eigen: float32 [2, 1024], P('mirror'), may hold values from 0.25 to 4
- wave_square: float32 [65536], P(('cols', 'slab')), parts along dimension 0, may hold values from 0.25 to 4
Outputs:
- solution: float32 [2, 1024, 65536], P('mirror', 'slab', 'cols'), parts along dimension 2
The draws below stay inside these ranges and needn't reach their ends.
There are 2 independent parts, one for each index of `cols`. The reference program is written for one: setup_inputs(seed, part) draws one part's arguments, and reference() takes and returns one part's arrays. A program takes and returns all parts, laid end to end along the dimension named above; an argument that names none is the same for every part. Nothing has to cross between parts.
All inputs are finite; a program needn't handle non-finite values.
Results may differ from the reference program's by a relative error of at most 0.0001.
Values sent between devices are 32-bit elements; how exact they have to be, the bound alone decides.
No kernel may reach another device: no remote copies, remote signals or barrier semaphores. Data moves between devices by JAX's collectives and lax.ppermute only.
A program may use at most 64 MiB of HBM per device.

```python
import math
import jax
import jax.numpy as jnp
from jax import lax

HALF = 1024
MODES = 32768


def levels(key, dims, shards, least, high):
    gain = 1.0
    for axis_at, parts in shards:
        heights = jax.random.uniform(jax.random.fold_in(jax.random.fold_in(key, 6), axis_at), (parts,), jnp.float32, least / len(shards), high / len(shards))
        gain = gain * jnp.repeat(jnp.exp(heights), dims[axis_at] // parts).reshape((-1,) + (1,) * (len(dims) - 1 - axis_at))
    return gain


def bell_draw(rng, dims, width, most, shards=(), held_as=jnp.bfloat16):
    result = width * jax.random.normal(rng, dims, jnp.float32)
    if shards:
        result = result * levels(rng, dims, shards, -0.22, 0.18)
    return jnp.clip(result, -most, most).astype(held_as)


def setup_inputs(seed: int = 0, part: int = 0) -> dict:
    key_list = jax.random.split(jax.random.key(seed), 6)
    part_keys = jax.random.split(jax.random.fold_in(key_list[5], part), 6)
    return {
        "right_side": bell_draw(part_keys[0], (2, HALF, MODES), 1.0, 6.0, ((0, 2), (1, 64)), jnp.float32),
        "analysis": bell_draw(key_list[1], (2, HALF, HALF), HALF ** -0.5, 0.1875, ((0, 2),), jnp.float32),
        "synthesis": bell_draw(key_list[2], (2, HALF, HALF), HALF ** -0.5, 0.1875, ((0, 2),), jnp.float32),
        "negated_eigen": jnp.clip(jnp.exp(math.log(4.0) - 2.7725887 * jax.random.uniform(key_list[3], (2, HALF), jnp.float32) ** levels(key_list[3], (2, HALF), ((0, 2),), -0.2, 0.2)), 0.25, 4.0),
        "wave_square": jnp.clip(jnp.exp(math.log(4.0) - 2.7725887 * jax.random.uniform(part_keys[4], (MODES,), jnp.float32) ** levels(part_keys[4], (MODES,), ((0, 64),), -0.2, 0.2)), 0.25, 4.0),
    }


def reference(right_side, analysis, synthesis, negated_eigen, wave_square):
    parity_fields = []
    for parity in range(2):
        folded = (right_side[0] + (1 - 2 * parity) * right_side[1]) * 0.5
        coefficients = jnp.dot(analysis[parity], folded, precision=lax.Precision.HIGHEST, preferred_element_type=jnp.float32)
        scaled = coefficients / (negated_eigen[parity][:, None] + wave_square[None, :])
        parity_fields.append(-jnp.dot(synthesis[parity], scaled, precision=lax.Precision.HIGHEST, preferred_element_type=jnp.float32))
    return jnp.stack((parity_fields[0] + parity_fields[1], parity_fields[0] - parity_fields[1]))
```

```python
import jax
import jax.numpy as jnp
from jax import lax
from jax.experimental import pallas as pl
from jax.experimental.pallas import tpu as pltpu
from jax.sharding import PartitionSpec as P


PLANE = ("mirror", "slab")
Z, YL, X = 8, 2, 4
INNER = YL * X
ROWS, COLS = 16, 256
POINTS = Z * INNER * ROWS
WIDE = Z * INNER * 2 * COLS
BLOCK = INNER * ROWS
HOPS = (0, 4, 3, 5, 2, 6, 1, 7)
MIB = 1024 * 1024
F32, BF16 = jnp.float32, jnp.bfloat16


def f32(*shape):
    return jax.ShapeDtypeStruct(shape, F32)


def call(kernel, inputs, outs, scratch=(), flops=0):
    spec = pl.BlockSpec(memory_space=pltpu.VMEM)
    size = sum(v.size * 4 for v in (*inputs, *outs))
    return pl.pallas_call(
        kernel,
        out_shape=tuple(outs),
        in_specs=[spec] * len(inputs),
        out_specs=tuple([spec] * len(outs)),
        scratch_shapes=list(scratch),
        compiler_params=pltpu.CompilerParams(vmem_limit_bytes=40 * MIB),
        cost_estimate=pl.CostEstimate(flops=flops, bytes_accessed=size, transcendentals=0),
    )(*inputs)


def place():
    return lax.axis_index("slab") >> 3


def sign():
    return (1 - 2 * lax.axis_index("mirror")).astype(F32)


def target(hop):
    return (place() + hop) & (Z - 1)


def source(hop):
    return (place() - hop) & (Z - 1)


def open_kernel(x_ref, plane_ref, *z_refs):
    for s in range(Z * INNER):
        z, i = s // INNER, s % INNER
        tile = x_ref[0, :, s * 2 * COLS : s * 2 * COLS + COLS]
        plane_ref[i, z] = tile
        plane_ref[INNER + i, z] = tile
    for hop, ref in zip(HOPS, z_refs):
        base = target(hop) * (INNER * 2 * COLS) + COLS
        for i in range(INNER):
            at = pl.multiple_of(base + i * 2 * COLS, COLS)
            ref[i] = x_ref[0, :, pl.ds(at, COLS)]


def plane_to_z_kernel(in_ref, *z_refs):
    flip = sign()
    for hop, ref in zip(HOPS, z_refs):
        z = target(hop)
        for i in range(INNER):
            ref[i] = in_ref[i, z] + flip * in_ref[INNER + i, z]


def z_to_plane_kernel(*refs):
    out_ref = refs[-1]
    for hop, ref in zip(HOPS, refs):
        z = source(hop)
        for i in range(INNER):
            tile = ref[i]
            out_ref[i, z] = tile
            out_ref[INNER + i, z] = tile


def split(value):
    high = value.astype(BF16)
    return high, (value - high.astype(F32)).astype(BF16)


def split_kernel(a_ref, s_ref, ah_ref, al_ref, sh_ref, sl_ref):
    @pl.loop(0, POINTS // 64)
    def _(step):
        rows = pl.ds(pl.multiple_of(step * 64, 64), 64)
        ah_ref[rows], al_ref[rows] = split(a_ref[0, rows])
        sh_ref[rows], sl_ref[rows] = split(s_ref[0, rows])


def product(high, low, high_ref, low_ref):
    def dot(a, b):
        return jnp.dot(a, b, preferred_element_type=F32)

    return dot(high, high_ref[...]) + (dot(high, low_ref[...]) + dot(low, high_ref[...]))


def solve(ah_ref, al_ref, sh_ref, sl_ref, neg_ref, wave, fh, fl, ch, cl, done):
    step_rows = 256

    @pl.loop(0, POINTS // step_rows)
    def _(step):
        rows = pl.ds(pl.multiple_of(step * step_rows, step_rows), step_rows)
        coefficients = product(ah_ref[rows], al_ref[rows], fh, fl)
        scaled = coefficients / (neg_ref[rows] + wave)
        ch[rows], cl[rows] = split(scaled)

    @pl.loop(0, POINTS // step_rows)
    def _(step):
        rows = pl.ds(pl.multiple_of(step * step_rows, step_rows), step_rows)
        done[rows] = -product(sh_ref[rows], sl_ref[rows], ch, cl)


def solve_z_kernel(*refs):
    matrices, neg_ref, wave_ref = refs[:4], refs[4], refs[5]
    ins, outs = refs[6:14], refs[14:22]
    fh, fl, ch, cl, done = refs[22:]
    for hop, ref in zip(HOPS, ins):
        rows = pl.ds(pl.multiple_of(source(hop) * BLOCK, BLOCK), BLOCK)
        fh[rows], fl[rows] = split(ref[...].reshape(BLOCK, COLS) * 0.5)
    solve(*matrices, neg_ref, wave_ref[:, :COLS], fh, fl, ch, cl, done)
    for hop, ref in zip(HOPS, outs):
        rows = pl.ds(pl.multiple_of(target(hop) * BLOCK, BLOCK), BLOCK)
        ref[...] = done[rows].reshape(INNER, ROWS, COLS)


def solve_plane_kernel(*refs):
    matrices, neg_ref, wave_ref = refs[:4], refs[4], refs[5]
    in_ref, out_ref = refs[6:8]
    fh, fl, ch, cl, done = refs[8:]
    flip = sign()
    for z in range(Z):
        for i in range(INNER):
            at = (z * INNER + i) * ROWS
            tile = (in_ref[i, z] + flip * in_ref[INNER + i, z]) * 0.5
            fh[at : at + ROWS], fl[at : at + ROWS] = split(tile)
    solve(*matrices, neg_ref, wave_ref[:, COLS:], fh, fl, ch, cl, done)
    for z in range(Z):
        for i in range(INNER):
            at = (z * INNER + i) * ROWS
            tile = done[at : at + ROWS]
            out_ref[i, z] = tile
            out_ref[INNER + i, z] = tile


def close_kernel(plane_ref, *refs):
    z_refs, out_ref, held, sems = refs[:Z], refs[Z], refs[Z + 1], refs[Z + 2]
    flip = sign()
    for hop, ref in zip(HOPS, z_refs):
        base = source(hop) * (INNER * 2 * COLS) + COLS
        for i in range(INNER):
            at = pl.multiple_of(base + i * 2 * COLS, COLS)
            held[:, pl.ds(at, COLS)] = ref[i]
    copies = []
    for z in range(Z):
        for i in range(INNER):
            at = (z * INNER + i) * 2 * COLS
            held[:, at : at + COLS] = plane_ref[i, z] + flip * plane_ref[INNER + i, z]
        cols = pl.ds(z * INNER * 2 * COLS, INNER * 2 * COLS)
        copies.append(pltpu.make_async_copy(held.at[:, cols], out_ref.at[0, :, cols], sems.at[z]))
        copies[-1].start()
    for copy in copies:
        copy.wait()


def plane_exchange(blocks, name):
    groups = [
        [m * Z * INNER + z * INNER + i for m in range(2) for i in range(INNER)] for z in range(Z)
    ]
    with jax.named_scope(name):
        return lax.all_to_all(
            blocks, PLANE, split_axis=0, concat_axis=0, axis_index_groups=groups, tiled=True
        )


def z_exchange(blocks, name):
    arrived = []
    for hop, block in zip(HOPS, blocks):
        if hop:
            pairs = [
                (z * INNER + i, (z + hop) % Z * INNER + i) for z in range(Z) for i in range(INNER)
            ]
            with jax.named_scope(f"{name}_{hop}"):
                block = lax.ppermute(block, "slab", pairs)
        arrived.append(block)
    return arrived


def shards(right_side, analysis, synthesis, negated_eigen, wave_square):
    block = f32(INNER, ROWS, COLS)
    plane = f32(2 * INNER, Z, ROWS, COLS)
    half = jax.ShapeDtypeStruct((POINTS, POINTS), BF16)
    work = [pltpu.VMEM((POINTS, COLS), BF16)] * 4 + [pltpu.VMEM((POINTS, COLS), F32)]
    flops = 12 * POINTS * POINTS * COLS

    plane_a, *z_b = call(open_kernel, [right_side], [plane] + [block] * Z)
    plane_a = plane_exchange(plane_a, "plane_a")
    z_b = z_exchange(z_b, "z_b")
    matrices = call(split_kernel, [analysis, synthesis], [half] * 4)
    levels = (*matrices, negated_eigen.reshape(POINTS, 1), wave_square.reshape(1, 2 * COLS))
    z_a = call(plane_to_z_kernel, [plane_a], [block] * Z)
    (plane_b,) = call(z_to_plane_kernel, z_b, [plane])
    plane_b = plane_exchange(plane_b, "plane_b")
    z_a = z_exchange(z_a, "z_a")
    z_a = call(solve_z_kernel, [*levels, *z_a], [block] * Z, work, flops)
    (plane_b,) = call(solve_plane_kernel, [*levels, plane_b], [plane], work, flops)
    z_a = z_exchange(z_a, "back_z_a")
    plane_b = plane_exchange(plane_b, "back_plane_b")
    z_b = call(plane_to_z_kernel, [plane_b], [block] * Z)
    (plane_a,) = call(z_to_plane_kernel, z_a, [plane])
    plane_a = plane_exchange(plane_a, "back_plane_a")
    z_b = z_exchange(z_b, "back_z_b")
    whole = f32(1, ROWS, WIDE)
    spec = pl.BlockSpec(memory_space=pltpu.VMEM)
    return pl.pallas_call(
        close_kernel,
        out_shape=whole,
        in_specs=[spec] * (1 + Z),
        out_specs=pl.BlockSpec(memory_space=pl.ANY),
        scratch_shapes=[pltpu.VMEM((ROWS, WIDE), F32), pltpu.SemaphoreType.DMA((Z,))],
        compiler_params=pltpu.CompilerParams(vmem_limit_bytes=40 * MIB),
    )(plane_a, *z_b)


def solution(mesh):
    return jax.shard_map(
        shards,
        mesh=mesh,
        in_specs=(
            P("mirror", "slab", "cols"),
            P("mirror", None, None),
            P("mirror", None, None),
            P("mirror", None),
            P(("cols", "slab")),
        ),
        out_specs=P("mirror", "slab", "cols"),
        check_vma=False,
    )
```

```python
import jax
import jax.numpy as jnp
from jax import lax
from jax.experimental import pallas as pl
from jax.experimental.pallas import tpu as pltpu
from jax.sharding import PartitionSpec as P


Z, YL, X = 8, 2, 4
ZX = Z * X
ROWS, COLS = 16, 256
POINTS = Z * YL * X * ROWS
WIDE = Z * YL * X * 2 * COLS
MIB = 1024 * 1024
F32, BF16 = jnp.float32, jnp.bfloat16
VMEM = pl.BlockSpec(memory_space=pltpu.VMEM)
ANY = pl.BlockSpec(memory_space=pltpu.HBM)
PART = jax.ShapeDtypeStruct((ZX, ROWS, COLS), F32)
WHOLE = jax.ShapeDtypeStruct((ZX, YL, ROWS, COLS), F32)
CHUNKS = 4
STEP = POINTS // CHUNKS
GRANT = 58


def call(kernel, inputs, outs, scratch=(), flops=0, grant=8, in_any=0, out_any=False):
    size = sum(v.size * 4 for v in (*inputs, *outs))
    return pl.pallas_call(
        kernel,
        out_shape=tuple(outs),
        in_specs=[ANY] * in_any + [VMEM] * (len(inputs) - in_any),
        out_specs=tuple([ANY if out_any else VMEM] * len(outs)),
        scratch_shapes=list(scratch),
        compiler_params=pltpu.CompilerParams(vmem_limit_bytes=grant * MIB),
        cost_estimate=pl.CostEstimate(flops=flops, bytes_accessed=size, transcendentals=0),
    )(*inputs)


def y_low():
    return (lax.axis_index("slab") >> 2) & 1


def signs():
    high, low = lax.axis_index("mirror"), y_low()
    own = 1 - 2 * high
    above = 1 - 2 * high * (1 - low)
    below = 1 - 2 * high * low
    return own.astype(F32), above.astype(F32), below.astype(F32)


def block_of(low, at):
    return (at // X) * YL * X + low * X + at % X


def open_kernel(x_hbm, b_ref, own_ref, other_ref, x_ref, sems):
    low = y_low()
    width = WIDE // CHUNKS
    copies = []
    for c in range(CHUNKS):
        cols = pl.ds(c * width, width)
        copies.append(pltpu.make_async_copy(x_hbm.at[:, :, cols], x_ref.at[:, :, cols], sems.at[c]))
        copies[-1].start()
    for at in range(ZX):
        if at % (ZX // CHUNKS) == 0:
            copies[at // (ZX // CHUNKS)].wait()
        for yl in range(YL):
            col = block_of(yl, at) * 2 * COLS
            b_ref[at, yl] = x_ref[0, :, col + COLS : col + 2 * COLS]
        base = (at // X) * YL * X + at % X
        for ref, half in ((own_ref, low), (other_ref, 1 - low)):
            col = pl.multiple_of((base + half * X) * 2 * COLS, COLS)
            ref[at] = x_ref[0, :, pl.ds(col, COLS)]


def pick_kernel(in_ref, own_ref, other_ref):
    low = y_low()
    for at in range(ZX):
        own_ref[at] = in_ref[at, low]
        other_ref[at] = in_ref[at, 1 - low]


def joined(own_ref, across_ref, above_ref, below_ref, at):
    own_sign, above_sign, below_sign = signs()
    near = across_ref[at] + own_sign * own_ref[at]
    far = above_sign * above_ref[at] + below_sign * below_ref[at]
    return near, far


def fold_kernel(own_ref, across_ref, above_ref, below_ref, out_ref):
    low = y_low()
    for at in range(ZX):
        near, far = joined(own_ref, across_ref, above_ref, below_ref, at)
        out_ref[at, low] = near
        out_ref[at, 1 - low] = far


def split(value):
    high = value.astype(BF16)
    return high, (value - high.astype(F32)).astype(BF16)


def split_kernel(a_ref, s_ref, *outs):
    @pl.loop(0, POINTS // 64)
    def _(step):
        rows = pl.ds(pl.multiple_of(step * 64, 64), 64)
        outs[0][rows], outs[1][rows] = split(a_ref[0, rows])
        outs[2][rows], outs[3][rows] = split(s_ref[0, rows])


def product(high, low, high_ref, low_ref):
    def dot(a, b):
        return jnp.dot(a, b, preferred_element_type=F32)

    return dot(high, high_ref[...]) + (dot(high, low_ref[...]) + dot(low, high_ref[...]))


def row_of(low, at):
    return block_of(low, at) * ROWS


def chunk(sources, held, sems, i, c):
    rows = pl.ds(pl.multiple_of(c * STEP, STEP), STEP)
    return pltpu.make_async_copy(sources[i].at[rows], held[i].at[rows], sems.at[i, c])


def fetch(sources, held, sems):
    for m in (0, 2):
        for c in range(CHUNKS):
            for i in (m, m + 1):
                chunk(sources, held, sems, i, c).start()


def solve(sources, held, sems, neg_ref, wave, fh, fl, ch, cl, done):
    @pl.loop(0, CHUNKS)
    def _(c):
        chunk(sources, held, sems, 0, c).wait()
        chunk(sources, held, sems, 1, c).wait()
        rows = pl.ds(pl.multiple_of(c * STEP, STEP), STEP)
        coefficients = product(held[0][rows], held[1][rows], fh, fl)
        ch[rows], cl[rows] = split(coefficients / (neg_ref[rows] + wave))

    @pl.loop(0, CHUNKS)
    def _(c):
        chunk(sources, held, sems, 2, c).wait()
        chunk(sources, held, sems, 3, c).wait()
        rows = pl.ds(pl.multiple_of(c * STEP, STEP), STEP)
        done[rows] = -product(held[2][rows], held[3][rows], ch, cl)


def solve_a_kernel(*refs):
    sources, (neg_ref, wave_ref, in_ref, out_ref) = refs[:4], refs[4:8]
    held, sems, work = refs[8:12], refs[12], refs[13:]
    fetch(sources, held, sems)
    fh, fl, _, _, done = work
    for at in range(ZX):
        for yl in range(YL):
            rows = pl.ds(row_of(yl, at), ROWS)
            fh[rows], fl[rows] = split(in_ref[at, yl] * 0.5)
    solve(sources, held, sems, neg_ref, wave_ref[:, :COLS], *work)
    for at in range(ZX):
        for yl in range(YL):
            out_ref[at, yl] = done[pl.ds(row_of(yl, at), ROWS)]


def solve_b_kernel(*refs):
    sources, (neg_ref, wave_ref, own_in, across, above, below) = refs[:4], refs[4:10]
    own_out, other_out = refs[10:12]
    held, sems, work = refs[12:16], refs[16], refs[17:]
    fetch(sources, held, sems)
    fh, fl, _, _, done = work
    low = y_low()

    def rows_of(half, at):
        base = ((at // X) * YL * X + at % X) * ROWS
        return pl.ds(pl.multiple_of(base + half * (X * ROWS), ROWS), ROWS)

    for at in range(ZX):
        near, far = joined(own_in, across, above, below, at)
        for half, value in ((low, near), (1 - low, far)):
            rows = rows_of(half, at)
            fh[rows], fl[rows] = split(value * 0.5)
    solve(sources, held, sems, neg_ref, wave_ref[:, COLS:], *work)
    for at in range(ZX):
        own_out[at] = done[rows_of(low, at)]
        other_out[at] = done[rows_of(1 - low, at)]


def close_kernel(b_ref, own_ref, across_ref, above_ref, below_ref, out_ref, held, sems):
    low = y_low()
    copies = []
    for z in range(Z):
        for at in range(z * X, z * X + X):
            near, far = joined(own_ref, across_ref, above_ref, below_ref, at)
            base = (at // X) * YL * X + at % X
            for half, value in ((low, near), (1 - low, far)):
                col = pl.multiple_of((base + half * X) * 2 * COLS, COLS)
                held[:, pl.ds(col, COLS)] = value
            for yl in range(YL):
                col = block_of(yl, at) * 2 * COLS + COLS
                held[:, col : col + COLS] = b_ref[at, yl]
        cols = pl.ds(z * YL * X * 2 * COLS, YL * X * 2 * COLS)
        copies.append(pltpu.make_async_copy(held.at[:, cols], out_ref.at[0, :, cols], sems.at[z]))
        copies[-1].start()
    for copy in copies:
        copy.wait()


def zx_exchange(blocks):
    groups = [[(z * YL + yl) * X + x for z in range(Z) for x in range(X)] for yl in range(YL)]
    return lax.all_to_all(
        blocks, "slab", split_axis=0, concat_axis=0, axis_index_groups=groups, tiled=True
    )


def y_move(block, hop):
    def device(y, z, x):
        return (y // YL) * Z * YL * X + (z * YL + y % YL) * X + x

    every = [(y, z, x) for y in range(2 * YL) for z in range(Z) for x in range(X)]
    pairs = [(device(y, z, x), device((y + hop) % 4, z, x)) for y, z, x in every]
    return lax.ppermute(block, ("mirror", "slab"), pairs)


def y_exchange(own, other):
    across = y_move(own, 2)
    above = y_move(other, 3)
    below = y_move(other, 1)
    return own, across, above, below


def body(right_side, analysis, synthesis, negated_eigen, wave_square):
    work = [
        *[pltpu.VMEM((POINTS, POINTS), BF16)] * 4,
        pltpu.SemaphoreType.DMA((4, CHUNKS)),
        *[pltpu.VMEM((POINTS, COLS), BF16)] * 4,
        pltpu.VMEM((POINTS, COLS), F32),
    ]
    flops = 12 * POINTS * POINTS * COLS
    half = jax.ShapeDtypeStruct((POINTS, POINTS), BF16)
    matrices = call(split_kernel, [analysis, synthesis], [half] * 4)
    levels = (*matrices, negated_eigen.reshape(POINTS, 1), wave_square.reshape(1, 2 * COLS))
    held = [pltpu.VMEM((ROWS, WIDE), F32), pltpu.SemaphoreType.DMA((Z,))]

    stage = [pltpu.VMEM((1, ROWS, WIDE), F32), pltpu.SemaphoreType.DMA((CHUNKS,))]

    b, *a = call(open_kernel, [right_side], [WHOLE, PART, PART], stage, 0, GRANT, 1)
    b = zx_exchange(b)
    a = y_exchange(*a)
    (a,) = call(fold_kernel, a, [WHOLE])
    b = call(pick_kernel, [b], [PART, PART])
    a = zx_exchange(a)
    b = y_exchange(*b)
    b = call(solve_b_kernel, [*levels, *b], [PART, PART], work, flops, GRANT, 4)
    (a,) = call(solve_a_kernel, [*levels, a], [WHOLE], work, flops, GRANT, 4)
    a = zx_exchange(a)
    b = y_exchange(*b)
    (b,) = call(fold_kernel, b, [WHOLE])
    a = call(pick_kernel, [a], [PART, PART])
    b = zx_exchange(b)
    a = y_exchange(*a)
    out = jax.ShapeDtypeStruct((1, ROWS, WIDE), F32)
    return call(close_kernel, [b, *a], [out], held, out_any=True)[0]


def solution(mesh):
    return jax.shard_map(
        body,
        mesh=mesh,
        in_specs=(
            P("mirror", "slab", "cols"),
            P("mirror", None, None),
            P("mirror", None, None),
            P("mirror", None),
            P(("cols", "slab")),
        ),
        out_specs=P("mirror", "slab", "cols"),
        check_vma=False,
    )
```

```python
import jax
import jax.numpy as jnp
from jax import lax
from jax.experimental import pallas as pl
from jax.experimental.pallas import tpu as pltpu
from jax.sharding import PartitionSpec as P


Z, YL, X = 8, 2, 4
ZX = Z * X
ROWS, COLS = 16, 256
POINTS = Z * YL * X * ROWS
WIDE = Z * YL * X * 2 * COLS
MIB = 1024 * 1024
F32, BF16 = jnp.float32, jnp.bfloat16
VMEM = pl.BlockSpec(memory_space=pltpu.VMEM)
ANY = pl.BlockSpec(memory_space=pltpu.HBM)
PART = jax.ShapeDtypeStruct((ZX, ROWS, COLS), F32)
WHOLE = jax.ShapeDtypeStruct((ZX, YL, ROWS, COLS), F32)
CHUNKS = 4
PIECES = 2
STEP = POINTS // PIECES
GRANT = 52
OPEN = 50


def call(kernel, inputs, outs, scratch=(), flops=0, grant=8, in_any=0, out_any=0):
    size = sum(v.size * 4 for v in (*inputs, *outs))
    return pl.pallas_call(
        kernel,
        out_shape=tuple(outs),
        in_specs=[ANY] * in_any + [VMEM] * (len(inputs) - in_any),
        out_specs=tuple([ANY] * out_any + [VMEM] * (len(outs) - out_any)),
        scratch_shapes=list(scratch),
        compiler_params=pltpu.CompilerParams(vmem_limit_bytes=grant * MIB),
        cost_estimate=pl.CostEstimate(flops=flops, bytes_accessed=size, transcendentals=0),
    )(*inputs)


def y_low():
    return (lax.axis_index("slab") >> 2) & 1


def signs():
    high, low = lax.axis_index("mirror"), y_low()
    own = 1 - 2 * high
    above = 1 - 2 * high * (1 - low)
    below = 1 - 2 * high * low
    return own.astype(F32), above.astype(F32), below.astype(F32)


def block_of(low, at):
    return (at // X) * YL * X + low * X + at % X


def open_kernel(x_hbm, b_hbm, own_ref, other_ref, x_ref, b_ref, in_sems, out_sems):
    low = y_low()
    width, part = WIDE // CHUNKS, ZX // CHUNKS
    arrivals, departures = [], []
    for c in range(CHUNKS):
        cols = pl.ds(c * width, width)
        source = x_hbm.at[:, :, cols]
        arrivals.append(pltpu.make_async_copy(source, x_ref.at[:, :, cols], in_sems.at[c]))
        arrivals[-1].start()
    for c in range(CHUNKS):
        arrivals[c].wait()
        for at in range(c * part, c * part + part):
            for yl in range(YL):
                col = block_of(yl, at) * 2 * COLS
                b_ref[at, yl] = x_ref[0, :, col + COLS : col + 2 * COLS]
        rows = pl.ds(c * part, part)
        departures.append(pltpu.make_async_copy(b_ref.at[rows], b_hbm.at[rows], out_sems.at[c]))
        departures[-1].start()
    for at in range(ZX):
        base = (at // X) * YL * X + at % X
        for ref, half in ((own_ref, low), (other_ref, 1 - low)):
            col = pl.multiple_of((base + half * X) * 2 * COLS, COLS)
            ref[at] = x_ref[0, :, pl.ds(col, COLS)]
    for copy in departures:
        copy.wait()


def pick_kernel(in_ref, own_ref, other_ref):
    low = y_low()
    for at in range(ZX):
        own_ref[at] = in_ref[at, low]
        other_ref[at] = in_ref[at, 1 - low]


def joined(own_ref, across_ref, above_ref, below_ref, at):
    own_sign, above_sign, below_sign = signs()
    near = across_ref[at] + own_sign * own_ref[at]
    far = above_sign * above_ref[at] + below_sign * below_ref[at]
    return near, far


def fold_kernel(own_ref, across_ref, above_ref, below_ref, out_ref):
    low = y_low()
    for at in range(ZX):
        near, far = joined(own_ref, across_ref, above_ref, below_ref, at)
        out_ref[at, low] = near
        out_ref[at, 1 - low] = far


def split(value):
    high = value.astype(BF16)
    return high, (value - high.astype(F32)).astype(BF16)


def split_kernel(a_ref, s_ref, *outs):
    @pl.loop(0, POINTS // 64)
    def _(step):
        rows = pl.ds(pl.multiple_of(step * 64, 64), 64)
        outs[0][rows], outs[1][rows] = split(a_ref[0, rows])
        outs[2][rows], outs[3][rows] = split(s_ref[0, rows])


def product(high, low, high_ref, low_ref):
    def dot(a, b):
        return jnp.dot(a, b, preferred_element_type=F32)

    return dot(high, high_ref[...]) + (dot(high, low_ref[...]) + dot(low, high_ref[...]))


def row_of(low, at):
    return block_of(low, at) * ROWS


def chunk(sources, held, sems, i, c):
    rows = pl.ds(pl.multiple_of(c * STEP, STEP), STEP)
    return pltpu.make_async_copy(sources[i].at[rows], held[i].at[rows], sems.at[i, c])


def fetch(sources, held, sems):
    for m in (0, 2):
        for c in range(PIECES):
            for i in (m, m + 1):
                chunk(sources, held, sems, i, c).start()


def solve(sources, held, sems, neg_ref, wave, fh, fl, ch, cl, done):
    @pl.loop(0, PIECES)
    def _(c):
        chunk(sources, held, sems, 0, c).wait()
        chunk(sources, held, sems, 1, c).wait()
        rows = pl.ds(pl.multiple_of(c * STEP, STEP), STEP)
        coefficients = product(held[0][rows], held[1][rows], fh, fl)
        ch[rows], cl[rows] = split(coefficients / (neg_ref[rows] + wave))

    @pl.loop(0, PIECES)
    def _(c):
        chunk(sources, held, sems, 2, c).wait()
        chunk(sources, held, sems, 3, c).wait()
        rows = pl.ds(pl.multiple_of(c * STEP, STEP), STEP)
        done[rows] = -product(held[2][rows], held[3][rows], ch, cl)


def solve_a_kernel(*refs):
    sources, (neg_ref, wave_ref, in_ref, out_ref) = refs[:4], refs[4:8]
    held, sems, work = refs[8:12], refs[12], refs[13:]
    fetch(sources, held, sems)
    fh, fl, _, _, done = work
    for at in range(ZX):
        for yl in range(YL):
            rows = pl.ds(row_of(yl, at), ROWS)
            fh[rows], fl[rows] = split(in_ref[at, yl] * 0.5)
    solve(sources, held, sems, neg_ref, wave_ref[:, :COLS], *work)
    for at in range(ZX):
        for yl in range(YL):
            out_ref[at, yl] = done[pl.ds(row_of(yl, at), ROWS)]


def solve_b_kernel(*refs):
    sources, (neg_ref, wave_ref, own_in, across, above, below) = refs[:4], refs[4:10]
    own_out, other_out = refs[10:12]
    held, sems, work = refs[12:16], refs[16], refs[17:]
    fetch(sources, held, sems)
    fh, fl, _, _, done = work
    low = y_low()

    def rows_of(half, at):
        base = ((at // X) * YL * X + at % X) * ROWS
        return pl.ds(pl.multiple_of(base + half * (X * ROWS), ROWS), ROWS)

    for at in range(ZX):
        near, far = joined(own_in, across, above, below, at)
        for half, value in ((low, near), (1 - low, far)):
            rows = rows_of(half, at)
            fh[rows], fl[rows] = split(value * 0.5)
    solve(sources, held, sems, neg_ref, wave_ref[:, COLS:], *work)
    for at in range(ZX):
        own_out[at] = done[rows_of(low, at)]
        other_out[at] = done[rows_of(1 - low, at)]


def close_kernel(b_ref, own_ref, across_ref, above_ref, below_ref, out_ref, held, sems):
    low = y_low()
    copies = []
    for z in range(Z):
        for at in range(z * X, z * X + X):
            near, far = joined(own_ref, across_ref, above_ref, below_ref, at)
            base = (at // X) * YL * X + at % X
            for half, value in ((low, near), (1 - low, far)):
                col = pl.multiple_of((base + half * X) * 2 * COLS, COLS)
                held[:, pl.ds(col, COLS)] = value
            for yl in range(YL):
                col = block_of(yl, at) * 2 * COLS + COLS
                held[:, col : col + COLS] = b_ref[at, yl]
        cols = pl.ds(z * YL * X * 2 * COLS, YL * X * 2 * COLS)
        copies.append(pltpu.make_async_copy(held.at[:, cols], out_ref.at[0, :, cols], sems.at[z]))
        copies[-1].start()
    for copy in copies:
        copy.wait()


def zx_exchange(blocks):
    groups = [[(z * YL + yl) * X + x for z in range(Z) for x in range(X)] for yl in range(YL)]
    return lax.all_to_all(
        blocks, "slab", split_axis=0, concat_axis=0, axis_index_groups=groups, tiled=True
    )


def y_move(block, hop):
    def device(y, z, x):
        return (y // YL) * Z * YL * X + (z * YL + y % YL) * X + x

    every = [(y, z, x) for y in range(2 * YL) for z in range(Z) for x in range(X)]
    pairs = [(device(y, z, x), device((y + hop) % 4, z, x)) for y, z, x in every]
    return lax.ppermute(block, ("mirror", "slab"), pairs)


def y_exchange(own, other):
    across = y_move(own, 2)
    above = y_move(other, 3)
    below = y_move(other, 1)
    return own, across, above, below


def body(right_side, analysis, synthesis, negated_eigen, wave_square):
    work = [
        *[pltpu.VMEM((POINTS, POINTS), BF16)] * 4,
        pltpu.SemaphoreType.DMA((4, PIECES)),
        *[pltpu.VMEM((POINTS, COLS), BF16)] * 4,
        pltpu.VMEM((POINTS, COLS), F32),
    ]
    flops = 12 * POINTS * POINTS * COLS
    half = jax.ShapeDtypeStruct((POINTS, POINTS), BF16)
    matrices = call(split_kernel, [analysis, synthesis], [half] * 4)
    levels = (*matrices, negated_eigen.reshape(POINTS, 1), wave_square.reshape(1, 2 * COLS))
    held = [pltpu.VMEM((ROWS, WIDE), F32), pltpu.SemaphoreType.DMA((Z,))]

    stage = [
        pltpu.VMEM((1, ROWS, WIDE), F32),
        pltpu.VMEM(WHOLE.shape, F32),
        *[pltpu.SemaphoreType.DMA((CHUNKS,))] * 2,
    ]

    b, *a = call(open_kernel, [right_side], [WHOLE, PART, PART], stage, 0, OPEN, 1, 1)
    b = zx_exchange(b)
    a = y_exchange(*a)
    (a,) = call(fold_kernel, a, [WHOLE])
    b = call(pick_kernel, [b], [PART, PART])
    a = zx_exchange(a)
    b = y_exchange(*b)
    b = call(solve_b_kernel, [*levels, *b], [PART, PART], work, flops, GRANT, 4)
    (a,) = call(solve_a_kernel, [*levels, a], [WHOLE], work, flops, GRANT, 4)
    a = zx_exchange(a)
    b = y_exchange(*b)
    (b,) = call(fold_kernel, b, [WHOLE])
    a = call(pick_kernel, [a], [PART, PART])
    b = zx_exchange(b)
    a = y_exchange(*a)
    out = jax.ShapeDtypeStruct((1, ROWS, WIDE), F32)
    return call(close_kernel, [b, *a], [out], held, out_any=1)[0]


def solution(mesh):
    return jax.shard_map(
        body,
        mesh=mesh,
        in_specs=(
            P("mirror", "slab", "cols"),
            P("mirror", None, None),
            P("mirror", None, None),
            P("mirror", None),
            P(("cols", "slab")),
        ),
        out_specs=P("mirror", "slab", "cols"),
        check_vma=False,
    )
```

```python
import jax
import jax.numpy as jnp
from jax import lax
from jax.experimental import pallas as pl
from jax.experimental.pallas import tpu as pltpu
from jax.sharding import PartitionSpec as P


Z, YL, X = 8, 2, 4
ZX = Z * X
ROWS, COLS = 16, 256
POINTS = Z * YL * X * ROWS
WIDE = Z * YL * X * 2 * COLS
MIB = 1024 * 1024
F32, BF16 = jnp.float32, jnp.bfloat16
VMEM = pl.BlockSpec(memory_space=pltpu.VMEM)
ANY = pl.BlockSpec(memory_space=pltpu.HBM)
PART = jax.ShapeDtypeStruct((ZX, ROWS, COLS), F32)
WHOLE = jax.ShapeDtypeStruct((ZX, YL, ROWS, COLS), F32)
CHUNKS = 4
PIECES = 2
STEP = POINTS // PIECES
GRANT = 52
OPEN = 50


def call(kernel, inputs, outs, scratch=(), flops=0, grant=8, in_any=0, out_any=0):
    size = sum(v.size * 4 for v in (*inputs, *outs))
    return pl.pallas_call(
        kernel,
        out_shape=tuple(outs),
        in_specs=[ANY] * in_any + [VMEM] * (len(inputs) - in_any),
        out_specs=tuple([ANY] * out_any + [VMEM] * (len(outs) - out_any)),
        scratch_shapes=list(scratch),
        compiler_params=pltpu.CompilerParams(vmem_limit_bytes=grant * MIB),
        cost_estimate=pl.CostEstimate(flops=flops, bytes_accessed=size, transcendentals=0),
    )(*inputs)


def y_low():
    return (lax.axis_index("slab") >> 2) & 1


def signs():
    high, low = lax.axis_index("mirror"), y_low()
    own = 1 - 2 * high
    above = 1 - 2 * high * (1 - low)
    below = 1 - 2 * high * low
    return own.astype(F32), above.astype(F32), below.astype(F32)


def block_of(low, at):
    return (at // X) * YL * X + low * X + at % X


def open_kernel(x_hbm, b_hbm, own_ref, other_ref, x_ref, b_ref, in_sems, out_sems):
    low = y_low()
    width, part = WIDE // CHUNKS, ZX // CHUNKS
    arrivals, departures = [], []
    for c in range(CHUNKS):
        cols = pl.ds(c * width, width)
        source = x_hbm.at[:, :, cols]
        arrivals.append(pltpu.make_async_copy(source, x_ref.at[:, :, cols], in_sems.at[c]))
        arrivals[-1].start()
    for c in range(CHUNKS):
        arrivals[c].wait()
        for at in range(c * part, c * part + part):
            for yl in range(YL):
                col = block_of(yl, at) * 2 * COLS
                b_ref[at, yl] = x_ref[0, :, col + COLS : col + 2 * COLS]
        rows = pl.ds(c * part, part)
        departures.append(pltpu.make_async_copy(b_ref.at[rows], b_hbm.at[rows], out_sems.at[c]))
        departures[-1].start()
    for at in range(ZX):
        base = (at // X) * YL * X + at % X
        for ref, half in ((own_ref, low), (other_ref, 1 - low)):
            col = pl.multiple_of((base + half * X) * 2 * COLS, COLS)
            ref[at] = x_ref[0, :, pl.ds(col, COLS)]
    for copy in departures:
        copy.wait()


def pick_kernel(in_ref, own_ref, other_ref):
    low = y_low()
    for at in range(ZX):
        own_ref[at] = in_ref[at, low]
        other_ref[at] = in_ref[at, 1 - low]


def joined(own_ref, across_ref, above_ref, below_ref, at):
    own_sign, above_sign, below_sign = signs()
    near = across_ref[at] + own_sign * own_ref[at]
    far = above_sign * above_ref[at] + below_sign * below_ref[at]
    return near, far


def fold_kernel(own_ref, across_ref, above_ref, below_ref, out_ref):
    low = y_low()
    for at in range(ZX):
        near, far = joined(own_ref, across_ref, above_ref, below_ref, at)
        out_ref[at, low] = near
        out_ref[at, 1 - low] = far


def split(value):
    high = value.astype(BF16)
    return high, (value - high.astype(F32)).astype(BF16)


def split_kernel(a_ref, s_ref, *outs):
    @pl.loop(0, POINTS // 64)
    def _(step):
        rows = pl.ds(pl.multiple_of(step * 64, 64), 64)
        outs[0][rows], outs[1][rows] = split(a_ref[0, rows])
        outs[2][rows], outs[3][rows] = split(s_ref[0, rows])


def product(high, low, high_ref, low_ref):
    def dot(a, b):
        return jnp.dot(a, b, preferred_element_type=F32)

    return dot(high, high_ref[...]) + (dot(high, low_ref[...]) + dot(low, high_ref[...]))


def row_of(low, at):
    return block_of(low, at) * ROWS


def chunk(sources, held, sems, i, c):
    rows = pl.ds(pl.multiple_of(c * STEP, STEP), STEP)
    return pltpu.make_async_copy(sources[i].at[rows], held[i].at[rows], sems.at[i, c])


def begin(sources, held, sems, m, c):
    chunk(sources, held, sems, m, c).start()
    chunk(sources, held, sems, m + 1, c).start()


def arrive(sources, held, sems, m, c):
    chunk(sources, held, sems, m, c).wait()
    chunk(sources, held, sems, m + 1, c).wait()


def fetch(sources, held, sems):
    for c in range(PIECES):
        begin(sources, held, sems, 0, c)


def solve(sources, held, sems, neg_ref, wave, fh, fl, ch, cl, done, ready=None):
    @pl.loop(0, PIECES)
    def _(c):
        arrive(sources, held, sems, 0, c)

        begin(sources, held, sems, 2, c)
        rows = pl.ds(pl.multiple_of(c * STEP, STEP), STEP)
        coefficients = product(held[0][rows], held[1][rows], fh, fl)
        ch[rows], cl[rows] = split(coefficients / (neg_ref[rows] + wave))

    @pl.loop(0, PIECES)
    def _(c):
        arrive(sources, held, sems, 2, c)
        rows = pl.ds(pl.multiple_of(c * STEP, STEP), STEP)
        done[rows] = -product(held[2][rows], held[3][rows], ch, cl)
        if ready is not None:
            ready(c)


def solve_a_kernel(*refs):
    sources, in_hbm, neg_ref, wave_ref, out_hbm = refs[:4], *refs[4:8]
    held, sems, work = refs[8:12], refs[12], refs[13:18]
    in_ref, out_ref, in_sems, out_sems = refs[18:]
    fh, fl, _, _, done = work
    part = ZX // PIECES
    arrivals = []
    for p in range(PIECES):
        ats = pl.ds(p * part, part)
        arrivals.append(pltpu.make_async_copy(in_hbm.at[ats], in_ref.at[ats], in_sems.at[p]))
        arrivals[-1].start()
    fetch(sources, held, sems)
    for at in range(ZX):
        if at % part == 0:
            arrivals[at // part].wait()
        for yl in range(YL):
            rows = pl.ds(row_of(yl, at), ROWS)
            fh[rows], fl[rows] = split(in_ref[at, yl] * 0.5)

    def leave(p):
        ats = pl.ds(pl.multiple_of(p * part, part), part)
        return pltpu.make_async_copy(out_ref.at[ats], out_hbm.at[ats], out_sems.at[p])

    def ready(p):
        base = p * part
        for i in range(part):
            for yl in range(YL):
                rows = pl.ds(pl.multiple_of(p * STEP + row_of(yl, i), ROWS), ROWS)
                out_ref[base + i, yl] = done[rows]
        leave(p).start()

    solve(sources, held, sems, neg_ref, wave_ref[:, :COLS], *work, ready)
    for p in range(PIECES):
        leave(p).wait()


def solve_b_kernel(*refs):
    sources, (neg_ref, wave_ref, own_in, across, above, below) = refs[:4], refs[4:10]
    own_out, other_out = refs[10:12]
    held, sems, work = refs[12:16], refs[16], refs[17:]
    fetch(sources, held, sems)
    fh, fl, _, _, done = work
    low = y_low()

    def rows_of(half, at):
        base = ((at // X) * YL * X + at % X) * ROWS
        return pl.ds(pl.multiple_of(base + half * (X * ROWS), ROWS), ROWS)

    for at in range(ZX):
        near, far = joined(own_in, across, above, below, at)
        for half, value in ((low, near), (1 - low, far)):
            rows = rows_of(half, at)
            fh[rows], fl[rows] = split(value * 0.5)
    solve(sources, held, sems, neg_ref, wave_ref[:, COLS:], *work)
    for at in range(ZX):
        own_out[at] = done[rows_of(low, at)]
        other_out[at] = done[rows_of(1 - low, at)]


def close_kernel(b_ref, own_ref, across_ref, above_ref, below_ref, out_ref, held, sems):
    low = y_low()
    copies = []
    for z in range(Z):
        for at in range(z * X, z * X + X):
            near, far = joined(own_ref, across_ref, above_ref, below_ref, at)
            base = (at // X) * YL * X + at % X
            for half, value in ((low, near), (1 - low, far)):
                col = pl.multiple_of((base + half * X) * 2 * COLS, COLS)
                held[:, pl.ds(col, COLS)] = value
            for yl in range(YL):
                col = block_of(yl, at) * 2 * COLS + COLS
                held[:, col : col + COLS] = b_ref[at, yl]
        cols = pl.ds(z * YL * X * 2 * COLS, YL * X * 2 * COLS)
        copies.append(pltpu.make_async_copy(held.at[:, cols], out_ref.at[0, :, cols], sems.at[z]))
        copies[-1].start()
    for copy in copies:
        copy.wait()


def zx_exchange(blocks):
    groups = [[(z * YL + yl) * X + x for z in range(Z) for x in range(X)] for yl in range(YL)]
    return lax.all_to_all(
        blocks, "slab", split_axis=0, concat_axis=0, axis_index_groups=groups, tiled=True
    )


def y_move(block, hop):
    def device(y, z, x):
        return (y // YL) * Z * YL * X + (z * YL + y % YL) * X + x

    every = [(y, z, x) for y in range(2 * YL) for z in range(Z) for x in range(X)]
    pairs = [(device(y, z, x), device((y + hop) % 4, z, x)) for y, z, x in every]
    return lax.ppermute(block, ("mirror", "slab"), pairs)


def y_exchange(own, other):
    across = y_move(own, 2)
    above = y_move(other, 3)
    below = y_move(other, 1)
    return own, across, above, below


def body(right_side, analysis, synthesis, negated_eigen, wave_square):
    work = [
        *[pltpu.VMEM((POINTS, POINTS), BF16)] * 4,
        pltpu.SemaphoreType.DMA((4, PIECES)),
        *[pltpu.VMEM((POINTS, COLS), BF16)] * 4,
        pltpu.VMEM((POINTS, COLS), F32),
    ]
    flops = 12 * POINTS * POINTS * COLS
    half = jax.ShapeDtypeStruct((POINTS, POINTS), BF16)
    matrices = call(split_kernel, [analysis, synthesis], [half] * 4)
    levels = (*matrices, negated_eigen.reshape(POINTS, 1), wave_square.reshape(1, 2 * COLS))
    held = [pltpu.VMEM((ROWS, WIDE), F32), pltpu.SemaphoreType.DMA((Z,))]

    stage = [
        pltpu.VMEM((1, ROWS, WIDE), F32),
        pltpu.VMEM(WHOLE.shape, F32),
        *[pltpu.SemaphoreType.DMA((CHUNKS,))] * 2,
    ]

    b, *a = call(open_kernel, [right_side], [WHOLE, PART, PART], stage, 0, OPEN, 1, 1)
    b = zx_exchange(b)
    a = y_exchange(*a)
    (a,) = call(fold_kernel, a, [WHOLE])
    b = call(pick_kernel, [b], [PART, PART])
    a = zx_exchange(a)
    b = y_exchange(*b)
    b = call(solve_b_kernel, [*levels, *b], [PART, PART], work, flops, GRANT, 4)
    inputs = [*matrices, a, *levels[4:]]
    own = [*[pltpu.VMEM(WHOLE.shape, F32)] * 2, *[pltpu.SemaphoreType.DMA((PIECES,))] * 2]
    (a,) = call(solve_a_kernel, inputs, [WHOLE], work + own, flops, GRANT, 5, 1)
    a = zx_exchange(a)
    b = y_exchange(*b)
    (b,) = call(fold_kernel, b, [WHOLE])
    a = call(pick_kernel, [a], [PART, PART])
    b = zx_exchange(b)
    a = y_exchange(*a)
    out = jax.ShapeDtypeStruct((1, ROWS, WIDE), F32)
    return call(close_kernel, [b, *a], [out], held, out_any=1)[0]


def solution(mesh):
    return jax.shard_map(
        body,
        mesh=mesh,
        in_specs=(
            P("mirror", "slab", "cols"),
            P("mirror", None, None),
            P("mirror", None, None),
            P("mirror", None),
            P(("cols", "slab")),
        ),
        out_specs=P("mirror", "slab", "cols"),
        check_vma=False,
    )
```
